256 devices in a mesh: blk: 16 (over y_hi, z), grp: 16 (over x, y_lo, core).
Axes of the slice: x: 4, y: 4 (y_hi: 2, y_lo: 2; y = y_hi * 2 + y_lo), z: 8, core: 2. Of those that a mesh axis runs over, the one named last changes fastest.
Arguments:
- history: bfloat16 [96, 32, 32768], P(None, None, ('blk', 'grp')), may hold values from -6 to 6
- delays: int32 [256, 256], P(('blk', 'grp')), may hold values from 0 to 92
- offsets: int32 [256, 256], P(('blk', 'grp')), may hold values from 0 to 7
- kernel: bfloat16 [32768, 32768], P(('blk', 'grp')), may hold values from -0.125 to 0.125
- incident: float32 [32, 32768], P(None, ('blk', 'grp')), may hold values from -6 to 6
- inverse: float32 [32768, 128], P(('blk', 'grp'))
Outputs:
- current: float32 [32, 32768], P(None, ('blk', 'grp'))
The draws below stay inside these ranges and needn't reach their ends.
All inputs are finite; a program needn't handle non-finite values.
Results may differ from the reference program's by a relative error of at most 0.0019.
Values may be sent and summed in bfloat16 or wider, within the bound.
A program may use at most 64 MiB of HBM per device.

```python
import math
import jax
import jax.numpy as jnp
import numpy as np
from jax import lax

ROWS = 128
EXC = 32
HIST = 96
ORDER = 4
FRAC = 8
BLOCKS = 256
UNKNOWNS = 32768


def draw_inverse(key, part):
    noise = jax.random.normal(key, (UNKNOWNS, ROWS), jnp.float32)
    position = jnp.arange(UNKNOWNS, dtype=jnp.int32) % ROWS
    identity = (position[:, None] == jnp.arange(ROWS, dtype=jnp.int32)[None, :]).astype(jnp.float32)
    return identity + 0.3 / math.sqrt(ROWS) * noise


def touch_ends(entries, own_key, smallest, largest):
    shape = entries.shape
    index_at = [jax.random.randint(jax.random.fold_in(own_key, axis), (), 0, shape[axis]) for axis in range(len(shape))]
    entries = entries.at[tuple(index_at)].set(smallest)
    longest = shape.index(max(shape))
    index_at[longest] = (index_at[longest] + 1) % shape[longest]
    return entries.at[tuple(index_at)].set(largest)


def strengthened(array, stream_key, source, target, blocks, factor):
    def block_of(axis_at):
        return (jnp.arange(array.shape[axis_at]) // (array.shape[axis_at] // blocks)).reshape((-1,) + (1,) * (array.ndim - 1 - axis_at))

    first = jax.random.permutation(stream_key, blocks)[block_of(target)]
    second = (block_of(target) + blocks // 2) % blocks
    return jnp.where((block_of(source) == first) | (block_of(source) == second), factor * array, array)


def shard_levels(key, dims, pieces, low, top_value):
    loudness = 1.0
    for axis_at, parts in pieces:
        draws = jax.random.uniform(jax.random.fold_in(jax.random.fold_in(key, 6), axis_at), (parts,), jnp.float32, low / len(pieces), top_value / len(pieces))
        loudness = loudness * jnp.repeat(jnp.exp(draws), dims[axis_at] // parts).reshape((-1,) + (1,) * (len(dims) - 1 - axis_at))
    return loudness


def scatter_about(key, shape, width, reach, split=(), kind=jnp.bfloat16):
    factor_of = shard_levels(key, shape, split, -0.22, 0.18) if split else 1.0
    entries = jax.random.normal(key, shape, jnp.float32) * width * factor_of
    return jnp.minimum(jnp.maximum(entries, -reach), reach).astype(kind)


def heavy_noise(stream_key, shape, spread, limit, pieces, heavy, kind=jnp.bfloat16):
    entries = spread * jax.random.normal(stream_key, shape, jnp.float32)
    if pieces:
        entries = entries * shard_levels(stream_key, shape, pieces, -0.22, 0.18)
    return jnp.clip(strengthened(entries, jax.random.fold_in(stream_key, 3), *heavy), -limit, limit).astype(kind)


def setup_inputs(seed: int = 0) -> dict:
    key_list = jax.random.split(jax.random.key(seed), 7)
    return {
        "history": scatter_about(key_list[0], (HIST, EXC, UNKNOWNS), 1.0, 6.0, ((2, 256),)),
        "delays": touch_ends(jax.random.randint(key_list[1], (BLOCKS, BLOCKS), 0, HIST - ORDER + 1), jax.random.fold_in(key_list[1], 1), 0, HIST - ORDER).astype(jnp.int32),
        "offsets": touch_ends(jax.random.randint(key_list[2], (BLOCKS, BLOCKS), 0, FRAC), jax.random.fold_in(key_list[2], 1), 0, FRAC - 1).astype(jnp.int32),
        "kernel": heavy_noise(key_list[3], (UNKNOWNS, UNKNOWNS), UNKNOWNS ** -0.5, 0.125, ((0, 256),), (1, 0, 256, 6.0)),
        "incident": scatter_about(key_list[4], (EXC, UNKNOWNS), 1.0, 6.0, ((1, 256),), jnp.float32),
        "inverse": draw_inverse(jax.random.fold_in(key_list[6], 71), 0),
    }


def weight_table():
    fractions = np.arange(FRAC) / FRAC
    node_list = np.arange(ORDER) - (ORDER // 2 - 1)
    lagrange = np.ones((FRAC, ORDER))
    for column in range(ORDER):
        for partner in range(ORDER):
            if partner != column:
                lagrange[:, column] = lagrange[:, column] * (fractions - node_list[partner]) / (node_list[column] - node_list[partner])
    return jnp.asarray(lagrange, jnp.float32)


def retarded(history_block, delay_row, offset_row, lagrange):
    window_rows = delay_row[:, None] + jnp.arange(ORDER, dtype=jnp.int32)[None, :]
    windows = jnp.take(history_block, window_rows, axis=0).astype(jnp.float32)
    chooser = (offset_row[:, None] == jnp.arange(FRAC, dtype=jnp.int32)[None, :]).astype(jnp.float32)
    weights = jnp.dot(chooser, lagrange, precision=lax.Precision.HIGHEST)
    slices = jnp.einsum("mp,mpqr->mqr", weights, windows, precision=lax.Precision.HIGHEST)
    return slices.astype(jnp.bfloat16)


def reference(history, delays, offsets, kernel, incident, inverse):
    lagrange = weight_table()
    block_count = delays.shape[0]
    excite_count = history.shape[1]
    kernel_grid = kernel.reshape(block_count, ROWS, block_count, ROWS)

    def one_source(summed, source):
        history_block = lax.dynamic_slice_in_dim(history, source * ROWS, ROWS, 2)
        delay_row = lax.dynamic_index_in_dim(delays, source, 0, keepdims=False)
        offset_row = lax.dynamic_index_in_dim(offsets, source, 0, keepdims=False)
        slices = retarded(history_block, delay_row, offset_row, lagrange)
        kernel_tiles = lax.dynamic_index_in_dim(kernel_grid, source, 2, keepdims=False)
        summed = summed + jnp.einsum("iqc,iac->qia", slices.astype(jnp.float32), kernel_tiles.astype(jnp.float32), precision=lax.Precision.HIGHEST)
        return summed, None

    initial = jnp.zeros((excite_count, block_count, ROWS), jnp.float32)
    summed, unused = lax.scan(one_source, initial, jnp.arange(block_count, dtype=jnp.int32))
    scattered = summed.reshape(excite_count, block_count * ROWS)
    rhs_field = incident - scattered
    inverse_grid = inverse.reshape(block_count, ROWS, ROWS)
    current = jnp.einsum("iac,qic->qia", inverse_grid, rhs_field.reshape(excite_count, block_count, ROWS), precision=lax.Precision.HIGHEST)
    return current.reshape(excite_count, block_count * ROWS)
```

```python
import jax
import jax.numpy as jnp
import numpy as np
from jax import lax
from jax.experimental import pallas as pl
from jax.experimental.pallas import tpu as pltpu
from jax.sharding import PartitionSpec as P

ORDER = 4
FRAC = 8
HIST = 96
EXC = 32
ROWS = 128
NDEV = 256
NZ = 8
PLANE = 32
DZ = (4, 3, -3, 2, -2, 1, -1, 0)
GROUPS = 8
PER = PLANE // GROUPS
MESH = pl.DeviceIdType.MESH


def weight_table():
    fractions = np.arange(FRAC) / FRAC
    node_list = np.arange(ORDER) - (ORDER // 2 - 1)
    lagrange = np.ones((FRAC, ORDER))
    for column in range(ORDER):
        for partner in range(ORDER):
            if partner != column:
                lagrange[:, column] = (
                    lagrange[:, column]
                    * (fractions - node_list[partner])
                    / (node_list[column] - node_list[partner])
                )
    return lagrange.astype(np.float32)


def device_of(x, y, z, c):
    return (y // 2) * NZ + z, x * 4 + (y % 2) * 2 + c


def body(
    delays, offsets, history, kernel, incident, inverse, out,
    table, past, tiles, send, recv, load_sem, tile_sem, send_sem, recv_sem,
):
    blk = lax.axis_index("blk")
    grp = lax.axis_index("grp")
    z = blk % NZ
    x = grp // 4
    y = (blk // NZ) * 2 + (grp // 2) % 2
    c = grp % 2

    def shifted(r, dz, sign):
        dc = r % 2
        dy = (r // 2) % 4
        dx = r // 8
        return device_of(
            (x + sign * dx + 4) % 4,
            (y + sign * dy + 4) % 4,
            (z + sign * dz + NZ) % NZ,
            (c + dc) % 2,
        )

    load = pltpu.make_async_copy(history, past, load_sem)
    load.start()
    fetch = pltpu.make_async_copy(kernel, tiles, tile_sem)
    fetch.start()

    barrier = pltpu.get_barrier_semaphore()

    def unless_self(r, dz, act):
        if dz == 0:
            pl.when(r != 0)(act)
        else:
            act()

    def greet(r, carry):
        for dz in DZ:
            def act():
                pl.semaphore_signal(
                    barrier, inc=1, device_id=shifted(r, dz, 1), device_id_type=MESH
                )
            unless_self(r, dz, act)
        return carry

    lax.fori_loop(0, PLANE, greet, 0)

    weights = weight_table()
    for s in range(FRAC):
        for p in range(ORDER):
            table[s, p] = jnp.float32(weights[s, p])
    load.wait()

    def interpolate(r, carry):
        for k, dz in enumerate(DZ):
            there = shifted(r, dz, 1)
            to = there[0] * 16 + there[1]
            first = delays[0, to]
            part = offsets[0, to]
            total = table[part, 0] * past[first].astype(jnp.float32)
            for p in range(1, ORDER):
                total += table[part, p] * past[first + p].astype(jnp.float32)
            send[r * NZ + k] = total.astype(jnp.bfloat16)
        return carry

    lax.fori_loop(0, PLANE, interpolate, 0)
    own = len(DZ) - 1
    recv[own] = send[own]

    pl.semaphore_wait(barrier, NDEV - 1)

    def ship(r, carry):
        for k, dz in enumerate(DZ):
            def act():
                slot = r * NZ + k
                pltpu.make_async_remote_copy(
                    src_ref=send.at[slot],
                    dst_ref=recv.at[slot],
                    send_sem=send_sem,
                    recv_sem=recv_sem.at[r // PER],
                    device_id=shifted(r, dz, 1),
                    device_id_type=MESH,
                ).start()
            unless_self(r, dz, act)
        return carry

    lax.fori_loop(0, PLANE, ship, 0)
    fetch.wait()

    total = jnp.zeros((EXC, ROWS), jnp.float32)
    for group in range(GROUPS):
        count = PER * NZ - (1 if group == 0 else 0)
        span = recv.at[pl.ds(group * PER * NZ, count)]
        pltpu.make_async_copy(span, span, recv_sem.at[group]).wait()

        def gather(pair, carry):
            r = group * PER + pair * 2
            for k, dz in enumerate(DZ):
                low = recv[(r + c) * NZ + k]
                high = recv[(r + 1 - c) * NZ + k]
                there = shifted(r, dz, -1)
                column = pl.multiple_of((there[0] * 16 + there[1] - c) * ROWS, 2 * ROWS)
                carry += lax.dot_general(
                    jnp.concatenate([low, high], axis=1),
                    tiles[:, pl.ds(column, 2 * ROWS)],
                    (((1,), (1,)), ((), ())),
                    preferred_element_type=jnp.float32,
                )
            return carry

        total = lax.fori_loop(0, PER // 2, gather, total)

    rhs_field = incident[...] - total
    out[...] = lax.dot_general(
        rhs_field,
        inverse[...],
        (((1,), (1,)), ((), ())),
        precision=lax.Precision.HIGHEST,
        preferred_element_type=jnp.float32,
    )
    sent = send.at[pl.ds(0, NDEV - 1)]
    pltpu.make_async_copy(sent, sent, send_sem).wait()


def per_device(history, delays, offsets, kernel, incident, inverse):
    smem = pl.BlockSpec(memory_space=pltpu.SMEM)
    vmem = pl.BlockSpec(memory_space=pltpu.VMEM)
    hbm = pl.BlockSpec(memory_space=pltpu.HBM)
    return pl.pallas_call(
        body,
        name="retarded_exchange",
        out_shape=jax.ShapeDtypeStruct((EXC, ROWS), jnp.float32),
        in_specs=[smem, smem, hbm, hbm, vmem, vmem],
        out_specs=vmem,
        scratch_shapes=[
            pltpu.SMEM((FRAC, ORDER), jnp.float32),
            pltpu.VMEM((HIST, EXC, ROWS), jnp.bfloat16),
            pltpu.VMEM((ROWS, NDEV * ROWS), jnp.bfloat16),
            pltpu.VMEM((NDEV, EXC, ROWS), jnp.bfloat16),
            pltpu.VMEM((NDEV, EXC, ROWS), jnp.bfloat16),
            pltpu.SemaphoreType.DMA,
            pltpu.SemaphoreType.DMA,
            pltpu.SemaphoreType.DMA,
            pltpu.SemaphoreType.DMA((GROUPS,)),
        ],
        compiler_params=pltpu.CompilerParams(
            collective_id=0, has_side_effects=True, vmem_limit_bytes=60 << 20
        ),
    )(delays, offsets, history, kernel, incident, inverse)


def solution(mesh):
    return jax.shard_map(
        per_device,
        mesh=mesh,
        in_specs=(
            P(None, None, ("blk", "grp")),
            P(("blk", "grp"), None),
            P(("blk", "grp"), None),
            P(("blk", "grp"), None),
            P(None, ("blk", "grp")),
            P(("blk", "grp"), None),
        ),
        out_specs=P(None, ("blk", "grp")),
        check_vma=False,
    )
```

```python
import jax
import jax.numpy as jnp
import numpy as np
from jax import lax
from jax.experimental import pallas as pl
from jax.experimental.pallas import tpu as pltpu
from jax.sharding import PartitionSpec as P

ORDER = 4
FRAC = 8
HIST = 96
EXC = 32
ROWS = 128
NDEV = 256
NX = 4
NY = 4
NZ = 8
MESH = pl.DeviceIdType.MESH


def hops(dx, dy, dz):
    return min(dx, NX - dx) + min(dy, NY - dy) + min(dz, NZ - dz)


PLANE = sorted(((dx, dy) for dx in range(NX) for dy in range(NY)), key=lambda d: hops(*d, 0))
CHIPS = [(dx, dy, dz) for dx, dy in PLANE for dz in range(NZ)]
FARTHEST = max(hops(*d) for d in CHIPS)
BY_HOPS = [
    sorted((d for d in CHIPS if hops(*d) == far), key=lambda d: -min(d[2], NZ - d[2]))
    for far in range(FARTHEST + 1)
]
SLOT = {d: 2 * n for n, d in enumerate(sum(BY_HOPS, []))}
GROUPS = ((0, 1), (2,), (3,), (4,), (5,), (6,), (7, 8))
GROUP_OF = {far: n for n, group in enumerate(GROUPS) for far in group}
PARTS = ((0, 1), (2,), (3, 4))
NEXT = ((1, 0, 0), (3, 0, 0), (0, 1, 0), (0, 3, 0), (0, 0, 1), (0, 0, 7))


def weight_table():
    fractions = np.arange(FRAC) / FRAC
    node_list = np.arange(ORDER) - (ORDER // 2 - 1)
    lagrange = np.ones((FRAC, ORDER))
    for column in range(ORDER):
        for partner in range(ORDER):
            if partner != column:
                lagrange[:, column] = (
                    lagrange[:, column]
                    * (fractions - node_list[partner])
                    / (node_list[column] - node_list[partner])
                )
    return lagrange.astype(np.float32)


def body(
    delays, offsets, history, kernel, incident, inverse, out,
    late, part_of, table, past, tiles, field, solve, send, recv,
    load_sem, send_sem, recv_sem, known_sem,
):
    blk = lax.axis_index("blk")
    grp = lax.axis_index("grp")
    z = blk % NZ
    x = grp // 4
    y = (blk // NZ) * 2 + (grp // 2) % 2
    c = grp % 2

    at_x = [((x + d) % NX) * 4 for d in range(NX)]
    ys = [(y + d) % NY for d in range(NY)]
    at_y = [((v // 2) * NZ, (v % 2) * 2) for v in ys]
    at_z = [(z + d) % NZ for d in range(NZ)]
    at_c = [c, 1 - c]

    def device(dx, dy, dz, dc):
        return at_y[dy][0] + at_z[dz], at_x[dx] + at_y[dy][1] + at_c[dc]

    def source_chip(dx, dy, dz):
        there = device(-dx % NX, -dy % NY, -dz % NZ, 0)
        return there[0] * 16 + there[1] - c

    def tell(sem, place):
        pl.semaphore_signal(sem, inc=1, device_id=device(*place), device_id_type=MESH)

    barrier = pltpu.get_barrier_semaphore()
    tell(barrier, (0, 0, 0, 1))
    for chip in NEXT:
        for dc in range(2):
            tell(barrier, (*chip, dc))

    loads = [
        pltpu.make_async_copy(source, target, load_sem.at[n])
        for n, (source, target) in enumerate(
            (
                (delays, late),
                (offsets, part_of),
                (history, past),
                (kernel, tiles),
                (incident, field),
                (inverse, solve),
            )
        )
    ]
    for load in loads:
        load.start()
    weights = weight_table()
    for s in range(FRAC):
        for p in range(ORDER):
            table[s, p] = jnp.float32(weights[s, p])
    for load in loads[:3]:
        load.wait()

    def interpolate(distances):
        plane = [d for d in PLANE if hops(*d, 0) in distances]

        def one_layer(dz, carry):
            for dx, dy in plane:
                for dc in range(2):
                    to = (at_y[dy][0] + (z + dz) % NZ) * 16 + at_x[dx] + at_y[dy][1] + at_c[dc]
                    first = late[0, to]
                    part = part_of[0, to]
                    total = table[part, 0] * past[first].astype(jnp.float32)
                    for p in range(1, ORDER):
                        total += table[part, p] * past[first + p].astype(jnp.float32)
                    send[((PLANE.index((dx, dy)) * NZ) + dz) * 2 + dc] = total.astype(jnp.bfloat16)
            return carry

        lax.fori_loop(0, NZ, one_layer, 0)

    def ship(far):
        for chip in BY_HOPS[far]:
            for dc in range(2):
                if (*chip, dc) == (0, 0, 0, 0):
                    continue
                start = (PLANE.index(chip[:2]) * NZ + chip[2]) * 2 + dc
                pltpu.make_async_remote_copy(
                    src_ref=send.at[start],
                    dst_ref=recv.at[SLOT[chip] + dc],
                    send_sem=send_sem,
                    recv_sem=recv_sem.at[GROUP_OF[far]],
                    device_id=device(*chip, dc),
                    device_id_type=MESH,
                ).start()

    for far in range(1, FARTHEST + 1):
        if far <= len(PARTS):
            interpolate(PARTS[far - 1])
        if far == 1:
            recv[SLOT[0, 0, 0]] = send[0]
            pl.semaphore_wait(barrier, 2 * len(NEXT) + 1)
        else:
            pl.semaphore_wait(known_sem.at[far], len(NEXT))
        if far < FARTHEST:
            for chip in NEXT:
                tell(known_sem.at[far + 1], (*chip, 0))
        if far == 1:
            ship(0)
        ship(far)

    for load in loads[3:]:
        load.wait()

    total = jnp.zeros((EXC, ROWS), jnp.float32)
    for n, group in enumerate(GROUPS):
        chips = [d for far in group for d in BY_HOPS[far]]
        count = 2 * len(chips) - (1 if 0 in group else 0)
        span = recv.at[pl.ds(SLOT[chips[0]] + (1 if 0 in group else 0), count)]
        pltpu.make_async_copy(span, span, recv_sem.at[n]).wait()
        for chip in chips:
            low = recv[SLOT[chip] + c]
            high = recv[SLOT[chip] + 1 - c]
            column = pl.multiple_of(source_chip(*chip) * ROWS, 2 * ROWS)
            total += lax.dot_general(
                jnp.concatenate([low, high], axis=1),
                tiles[:, pl.ds(column, 2 * ROWS)],
                (((1,), (1,)), ((), ())),
                preferred_element_type=jnp.float32,
            )

    out[...] = lax.dot_general(
        field[...] - total,
        solve[...],
        (((1,), (1,)), ((), ())),
        precision=lax.Precision.HIGHEST,
        preferred_element_type=jnp.float32,
    )
    sent = send.at[pl.ds(1, NDEV - 1)]
    pltpu.make_async_copy(sent, sent, send_sem).wait()


def per_device(history, delays, offsets, kernel, incident, inverse):
    hbm = pl.BlockSpec(memory_space=pltpu.HBM)
    return pl.pallas_call(
        body,
        name="retarded_exchange",
        out_shape=jax.ShapeDtypeStruct((EXC, ROWS), jnp.float32),
        in_specs=[hbm] * 6,
        out_specs=pl.BlockSpec(memory_space=pltpu.VMEM),
        scratch_shapes=[
            pltpu.SMEM((1, NDEV), jnp.int32),
            pltpu.SMEM((1, NDEV), jnp.int32),
            pltpu.SMEM((FRAC, ORDER), jnp.float32),
            pltpu.VMEM((HIST, EXC, ROWS), jnp.bfloat16),
            pltpu.VMEM((ROWS, NDEV * ROWS), jnp.bfloat16),
            pltpu.VMEM((EXC, ROWS), jnp.float32),
            pltpu.VMEM((ROWS, ROWS), jnp.float32),
            pltpu.VMEM((NDEV, EXC, ROWS), jnp.bfloat16),
            pltpu.VMEM((NDEV, EXC, ROWS), jnp.bfloat16),
            pltpu.SemaphoreType.DMA((6,)),
            pltpu.SemaphoreType.DMA,
            pltpu.SemaphoreType.DMA((len(GROUPS),)),
            pltpu.SemaphoreType.REGULAR((FARTHEST + 1,)),
        ],
        compiler_params=pltpu.CompilerParams(
            collective_id=0, has_side_effects=True, vmem_limit_bytes=60 << 20
        ),
    )(delays, offsets, history, kernel, incident, inverse)


def solution(mesh):
    return jax.shard_map(
        per_device,
        mesh=mesh,
        in_specs=(
            P(None, None, ("blk", "grp")),
            P(("blk", "grp"), None),
            P(("blk", "grp"), None),
            P(("blk", "grp"), None),
            P(None, ("blk", "grp")),
            P(("blk", "grp"), None),
        ),
        out_specs=P(None, ("blk", "grp")),
        check_vma=False,
    )
```

```python
import jax
import jax.numpy as jnp
import numpy as np
from jax import lax
from jax.experimental import pallas as pl
from jax.experimental.pallas import tpu as pltpu
from jax.sharding import PartitionSpec as P

ORDER = 4
FRAC = 8
HIST = 96
EXC = 32
ROWS = 128
NDEV = 256
NX = 4
NY = 4
NZ = 8
MESH = pl.DeviceIdType.MESH


def hops(dx, dy, dz):
    return min(dx, NX - dx) + min(dy, NY - dy) + min(dz, NZ - dz)


PLANE = sorted(((dx, dy) for dx in range(NX) for dy in range(NY)), key=lambda d: hops(*d, 0))
CHIPS = [(dx, dy, dz) for dx, dy in PLANE for dz in range(NZ)]
FARTHEST = max(hops(*d) for d in CHIPS)
def make_plan():
    def long_way(d):
        return min(d[2], NZ - d[2])

    def ring(far, sign):
        return sorted((d for d in CHIPS if hops(*d) == far), key=lambda d: sign * long_way(d))

    return [ring(0, 1) + ring(1, -1), ring(2, -1), ring(3, 1) + ring(4, 1), ring(5, 1) + ring(6, 1) + ring(7, 1) + ring(8, 1)]


LEAD = (2, 4)
NEXT = ((1, 0, 0), (3, 0, 0), (0, 1, 0), (0, 3, 0), (0, 0, 1), (0, 0, 7))
TELLERS = (NEXT, NEXT, tuple(d for d in CHIPS if hops(*d) == 2), ((2, 2, 0), (0, 0, 4)))
PLAN = make_plan()
ORDERED = sum(PLAN, [])
assert sorted(ORDERED) == sorted(CHIPS)
SLOT = {d: 2 * n for n, d in enumerate(ORDERED)}
SIZES = (8, 20, 24, 24, 24, 16, 8, 4)
ENDS = [sum(SIZES[:n + 1]) for n in range(len(SIZES))]
GROUPS = [ORDERED[end - size:end] for size, end in zip(SIZES, ENDS)]
GROUP_OF = {d: n for n, group in enumerate(GROUPS) for d in group}
PARTS = ((0, 1), (2,), (3, 4))


def weight_table():
    fractions = np.arange(FRAC) / FRAC
    node_list = np.arange(ORDER) - (ORDER // 2 - 1)
    lagrange = np.ones((FRAC, ORDER))
    for column in range(ORDER):
        for partner in range(ORDER):
            if partner != column:
                lagrange[:, column] = (
                    lagrange[:, column]
                    * (fractions - node_list[partner])
                    / (node_list[column] - node_list[partner])
                )
    return lagrange.astype(np.float32)


def body(
    delays, offsets, history, kernel, incident, inverse, out,
    late, part_of, table, past, tiles, field, solve, send, recv,
    load_sem, send_sem, recv_sem, known_sem,
):
    blk = lax.axis_index("blk")
    grp = lax.axis_index("grp")
    z = blk % NZ
    x = grp // 4
    y = (blk // NZ) * 2 + (grp // 2) % 2
    c = grp % 2

    at_x = [((x + d) % NX) * 4 for d in range(NX)]
    ys = [(y + d) % NY for d in range(NY)]
    at_y = [((v // 2) * NZ, (v % 2) * 2) for v in ys]
    at_z = [(z + d) % NZ for d in range(NZ)]
    at_c = [c, 1 - c]

    def device(dx, dy, dz, dc):
        return at_y[dy][0] + at_z[dz], at_x[dx] + at_y[dy][1] + at_c[dc]

    def source_chip(dx, dy, dz):
        there = device(-dx % NX, -dy % NY, -dz % NZ, 0)
        return there[0] * 16 + there[1] - c

    def tell(sem, place):
        pl.semaphore_signal(sem, inc=1, device_id=device(*place), device_id_type=MESH)

    barrier = pltpu.get_barrier_semaphore()
    tell(barrier, (0, 0, 0, 1))
    for chip in NEXT:
        for dc in range(2):
            tell(barrier, (*chip, dc))

    loads = [
        pltpu.make_async_copy(source, target, load_sem.at[n])
        for n, (source, target) in enumerate(
            (
                (delays, late),
                (offsets, part_of),
                (history, past),
                (kernel, tiles),
                (incident, field),
                (inverse, solve),
            )
        )
    ]
    for load in loads:
        load.start()
    weights = weight_table()
    for s in range(FRAC):
        for p in range(ORDER):
            table[s, p] = jnp.float32(weights[s, p])
    for load in loads[:3]:
        load.wait()

    def interpolate(distances):
        plane = [d for d in PLANE if hops(*d, 0) in distances]

        def one_layer(dz, carry):
            for dx, dy in plane:
                for dc in range(2):
                    to = (at_y[dy][0] + (z + dz) % NZ) * 16 + at_x[dx] + at_y[dy][1] + at_c[dc]
                    first = late[0, to]
                    part = part_of[0, to]
                    total = table[part, 0] * past[first].astype(jnp.float32)
                    for p in range(1, ORDER):
                        total += table[part, p] * past[first + p].astype(jnp.float32)
                    send[((PLANE.index((dx, dy)) * NZ) + dz) * 2 + dc] = total.astype(jnp.bfloat16)
            return carry

        lax.fori_loop(0, NZ, one_layer, 0)

    lead_x = [jnp.minimum((x + d) % NX, 2) for d in range(NX)]
    lead_y = [jnp.minimum(v, 2) for v in ys]
    lead_z = [v + NZ * (v // 4) for v in at_z]

    def send_to(chip):
        for dc in range(2):
            if (*chip, dc) == (0, 0, 0, 0):
                continue
            start = (PLANE.index(chip[:2]) * NZ + chip[2]) * 2 + dc
            pltpu.make_async_remote_copy(
                src_ref=send.at[start],
                dst_ref=recv.at[SLOT[chip] + dc],
                send_sem=send_sem,
                recv_sem=recv_sem.at[GROUP_OF[chip]],
                device_id=device(*chip, dc),
                device_id_type=MESH,
            ).start()

    def ship(stage):
        if stage + 1 < len(PLAN):
            for chip in PLAN[stage]:
                send_to(chip)
            return
        for tier in range(len(LEAD) + 1):
            for chip in PLAN[stage]:
                dx, dy, dz = chip
                lead = lead_x[dx] + lead_y[dy] + lead_z[dz]
                if tier == 0:
                    ahead = lead <= LEAD[0]
                elif tier == len(LEAD):
                    ahead = lead > LEAD[-1]
                else:
                    ahead = jnp.logical_and(lead > LEAD[tier - 1], lead <= LEAD[tier])

                @pl.when(ahead)
                def _():
                    send_to(chip)

    for stage, tellers in enumerate(TELLERS):
        if stage < len(PARTS):
            interpolate(PARTS[stage])
        if stage == 0:
            recv[SLOT[0, 0, 0]] = send[0]
            pl.semaphore_wait(barrier, 2 * len(NEXT) + 1)
        else:
            pl.semaphore_wait(known_sem.at[stage], len(tellers))
        if stage + 1 < len(TELLERS):
            for chip in TELLERS[stage + 1]:
                tell(known_sem.at[stage + 1], (*chip, 0))
        ship(stage)

    for load in loads[3:]:
        load.wait()

    total = jnp.zeros((EXC, ROWS), jnp.float32)
    for n, chips in enumerate(GROUPS):
        own = 1 if (0, 0, 0) in chips else 0
        span = recv.at[pl.ds(SLOT[chips[0]] + own, 2 * len(chips) - own)]
        pltpu.make_async_copy(span, span, recv_sem.at[n]).wait()
        for chip in chips:
            low = recv[SLOT[chip] + c]
            high = recv[SLOT[chip] + 1 - c]
            column = pl.multiple_of(source_chip(*chip) * ROWS, 2 * ROWS)
            total += lax.dot_general(
                jnp.concatenate([low, high], axis=1),
                tiles[:, pl.ds(column, 2 * ROWS)],
                (((1,), (1,)), ((), ())),
                preferred_element_type=jnp.float32,
            )

    out[...] = lax.dot_general(
        field[...] - total,
        solve[...],
        (((1,), (1,)), ((), ())),
        precision=lax.Precision.HIGHEST,
        preferred_element_type=jnp.float32,
    )
    sent = send.at[pl.ds(1, NDEV - 1)]
    pltpu.make_async_copy(sent, sent, send_sem).wait()


def per_device(history, delays, offsets, kernel, incident, inverse):
    hbm = pl.BlockSpec(memory_space=pltpu.HBM)
    return pl.pallas_call(
        body,
        name="retarded_exchange",
        out_shape=jax.ShapeDtypeStruct((EXC, ROWS), jnp.float32),
        in_specs=[hbm] * 6,
        out_specs=pl.BlockSpec(memory_space=pltpu.VMEM),
        scratch_shapes=[
            pltpu.SMEM((1, NDEV), jnp.int32),
            pltpu.SMEM((1, NDEV), jnp.int32),
            pltpu.SMEM((FRAC, ORDER), jnp.float32),
            pltpu.VMEM((HIST, EXC, ROWS), jnp.bfloat16),
            pltpu.VMEM((ROWS, NDEV * ROWS), jnp.bfloat16),
            pltpu.VMEM((EXC, ROWS), jnp.float32),
            pltpu.VMEM((ROWS, ROWS), jnp.float32),
            pltpu.VMEM((NDEV, EXC, ROWS), jnp.bfloat16),
            pltpu.VMEM((NDEV, EXC, ROWS), jnp.bfloat16),
            pltpu.SemaphoreType.DMA((6,)),
            pltpu.SemaphoreType.DMA,
            pltpu.SemaphoreType.DMA((len(GROUPS),)),
            pltpu.SemaphoreType.REGULAR((len(TELLERS),)),
        ],
        compiler_params=pltpu.CompilerParams(
            collective_id=0, has_side_effects=True, vmem_limit_bytes=60 << 20
        ),
    )(delays, offsets, history, kernel, incident, inverse)


def solution(mesh):
    return jax.shard_map(
        per_device,
        mesh=mesh,
        in_specs=(
            P(None, None, ("blk", "grp")),
            P(("blk", "grp"), None),
            P(("blk", "grp"), None),
            P(("blk", "grp"), None),
            P(None, ("blk", "grp")),
            P(("blk", "grp"), None),
        ),
        out_specs=P(None, ("blk", "grp")),
        check_vma=False,
    )
```

```python
import jax
import jax.numpy as jnp
import numpy as np
from jax import lax
from jax.experimental import pallas as pl
from jax.experimental.pallas import tpu as pltpu
from jax.sharding import PartitionSpec as P

ORDER = 4
FRAC = 8
HIST = 96
EXC = 32
ROWS = 128
NDEV = 256
NX = 4
NY = 4
NZ = 8
MESH = pl.DeviceIdType.MESH


def hops(dx, dy, dz):
    return min(dx, NX - dx) + min(dy, NY - dy) + min(dz, NZ - dz)


PLANE = sorted(((dx, dy) for dx in range(NX) for dy in range(NY)), key=lambda d: hops(*d, 0))
CHIPS = [(dx, dy, dz) for dx, dy in PLANE for dz in range(NZ)]
FARTHEST = max(hops(*d) for d in CHIPS)
def make_plan():
    def long_way(d):
        return min(d[2], NZ - d[2])

    def ring(far, sign):
        return sorted((d for d in CHIPS if hops(*d) == far), key=lambda d: sign * long_way(d))

    return [ring(0, 1) + ring(1, -1), ring(2, -1), ring(3, 1) + ring(4, 1), ring(5, 1) + ring(6, 1) + ring(7, 1) + ring(8, 1)]


LEAD = (2, 4)
NEXT = ((1, 0, 0), (3, 0, 0), (0, 1, 0), (0, 3, 0), (0, 0, 1), (0, 0, 7))
TELLERS = (NEXT, NEXT, tuple(d for d in CHIPS if hops(*d) == 2), ((2, 2, 0), (0, 0, 4)))
PLAN = make_plan()
ORDERED = sum(PLAN, [])
assert sorted(ORDERED) == sorted(CHIPS)
SLOT = {d: 2 * n for n, d in enumerate(ORDERED)}
SIZES = (8, 20, 24, 24, 24, 16, 8, 4)
ENDS = [sum(SIZES[:n + 1]) for n in range(len(SIZES))]
GROUPS = [ORDERED[end - size:end] for size, end in zip(SIZES, ENDS)]
GROUP_OF = {d: n for n, group in enumerate(GROUPS) for d in group}
PARTS = ((0, 1), (2,), (3, 4))


def weight_table():
    fractions = np.arange(FRAC) / FRAC
    node_list = np.arange(ORDER) - (ORDER // 2 - 1)
    lagrange = np.ones((FRAC, ORDER))
    for column in range(ORDER):
        for partner in range(ORDER):
            if partner != column:
                lagrange[:, column] = (
                    lagrange[:, column]
                    * (fractions - node_list[partner])
                    / (node_list[column] - node_list[partner])
                )
    return lagrange.astype(np.float32)


def body(
    delays, offsets, history, kernel, incident, inverse, out,
    late, part_of, table, past, tiles, field, solve, send, recv,
    load_sem, send_sem, recv_sem, known_sem,
):
    blk = lax.axis_index("blk")
    grp = lax.axis_index("grp")
    z = blk % NZ
    x = grp // 4
    y = (blk // NZ) * 2 + (grp // 2) % 2
    c = grp % 2

    at_x = [((x + d) % NX) * 4 for d in range(NX)]
    ys = [(y + d) % NY for d in range(NY)]
    at_y = [((v // 2) * NZ, (v % 2) * 2) for v in ys]
    at_z = [(z + d) % NZ for d in range(NZ)]
    at_c = [c, 1 - c]

    def device(dx, dy, dz, dc):
        return at_y[dy][0] + at_z[dz], at_x[dx] + at_y[dy][1] + at_c[dc]

    def source_chip(dx, dy, dz):
        there = device(-dx % NX, -dy % NY, -dz % NZ, 0)
        return there[0] * 16 + there[1] - c

    def tell(sem, place):
        pl.semaphore_signal(sem, inc=1, device_id=device(*place), device_id_type=MESH)

    barrier = pltpu.get_barrier_semaphore()
    tell(barrier, (0, 0, 0, 1))
    for chip in NEXT:
        for dc in range(2):
            tell(barrier, (*chip, dc))

    loads = [
        pltpu.make_async_copy(source, target, load_sem.at[n])
        for n, (source, target) in enumerate(
            (
                (delays, late),
                (offsets, part_of),
                (history, past),
                (kernel, tiles),
                (incident, field),
                (inverse, solve),
            )
        )
    ]
    for load in loads:
        load.start()
    weights = weight_table()
    for s in range(FRAC):
        for p in range(ORDER):
            table[s, p] = jnp.float32(weights[s, p])
    for load in loads[:3]:
        load.wait()

    def interpolate(distances):
        plane = [d for d in PLANE if hops(*d, 0) in distances]

        def one_layer(dz, carry):
            for dx, dy in plane:
                for dc in range(2):
                    to = (at_y[dy][0] + (z + dz) % NZ) * 16 + at_x[dx] + at_y[dy][1] + at_c[dc]
                    first = late[0, to]
                    part = part_of[0, to]
                    total = table[part, 0] * past[first].astype(jnp.float32)
                    for p in range(1, ORDER):
                        total += table[part, p] * past[first + p].astype(jnp.float32)
                    send[((PLANE.index((dx, dy)) * NZ) + dz) * 2 + dc] = total.astype(jnp.bfloat16)
            return carry

        lax.fori_loop(0, NZ, one_layer, 0)

    lead_x = [jnp.minimum((x + d) % NX, 2) for d in range(NX)]
    lead_y = [jnp.minimum(v, 2) for v in ys]
    lead_z = [v + NZ * (v // 4) for v in at_z]

    def send_to(chip):
        for dc in range(2):
            if (*chip, dc) == (0, 0, 0, 0):
                continue
            start = (PLANE.index(chip[:2]) * NZ + chip[2]) * 2 + dc
            pltpu.make_async_remote_copy(
                src_ref=send.at[start],
                dst_ref=recv.at[SLOT[chip] + dc],
                send_sem=send_sem,
                recv_sem=recv_sem.at[GROUP_OF[chip]],
                device_id=device(*chip, dc),
                device_id_type=MESH,
            ).start()

    def ship(stage):
        if stage + 1 < len(PLAN):
            for chip in PLAN[stage]:
                send_to(chip)
            return
        for tier in range(len(LEAD) + 1):
            for chip in PLAN[stage]:
                dx, dy, dz = chip
                lead = lead_x[dx] + lead_y[dy] + lead_z[dz]
                if tier == 0:
                    ahead = lead <= LEAD[0]
                elif tier == len(LEAD):
                    ahead = lead > LEAD[-1]
                else:
                    ahead = jnp.logical_and(lead > LEAD[tier - 1], lead <= LEAD[tier])

                @pl.when(ahead)
                def _():
                    send_to(chip)

    for stage, tellers in enumerate(TELLERS):
        if stage < len(PARTS):
            interpolate(PARTS[stage])
        if stage == 0:
            recv[SLOT[0, 0, 0]] = send[0]
            pl.semaphore_wait(barrier, 2 * len(NEXT) + 1)
        else:
            pl.semaphore_wait(known_sem.at[stage], len(tellers))
        if stage + 1 < len(TELLERS):
            for chip in TELLERS[stage + 1]:
                tell(known_sem.at[stage + 1], (*chip, 0))
        ship(stage)

    for load in loads[3:]:
        load.wait()

    total = jnp.zeros((EXC, ROWS), jnp.float32)
    for n, chips in enumerate(GROUPS):
        own = 1 if (0, 0, 0) in chips else 0
        span = recv.at[pl.ds(SLOT[chips[0]] + own, 2 * len(chips) - own)]
        pltpu.make_async_copy(span, span, recv_sem.at[n]).wait()
        for chip in chips:
            low = recv[SLOT[chip] + c]
            high = recv[SLOT[chip] + 1 - c]
            column = pl.multiple_of(source_chip(*chip) * ROWS, 2 * ROWS)
            total += lax.dot_general(
                jnp.concatenate([low, high], axis=1),
                tiles[:, pl.ds(column, 2 * ROWS)],
                (((1,), (1,)), ((), ())),
                preferred_element_type=jnp.float32,
            )

    out[...] = lax.dot_general(
        field[...] - total,
        solve[...],
        (((1,), (1,)), ((), ())),
        precision=lax.Precision.HIGHEST,
        preferred_element_type=jnp.float32,
    )
    sent = send.at[pl.ds(1, NDEV - 1)]
    pltpu.make_async_copy(sent, sent, send_sem).wait()


def per_device(history, delays, offsets, kernel, incident, inverse):
    hbm = pl.BlockSpec(memory_space=pltpu.HBM)
    args = [
        pltpu.with_memory_space_constraint(a, pltpu.HBM)
        for a in (delays, offsets, history, kernel, incident, inverse)
    ]
    return pl.pallas_call(
        body,
        name="retarded_exchange",
        out_shape=jax.ShapeDtypeStruct((EXC, ROWS), jnp.float32),
        in_specs=[hbm] * 6,
        out_specs=pl.BlockSpec(memory_space=pltpu.VMEM),
        scratch_shapes=[
            pltpu.SMEM((1, NDEV), jnp.int32),
            pltpu.SMEM((1, NDEV), jnp.int32),
            pltpu.SMEM((FRAC, ORDER), jnp.float32),
            pltpu.VMEM((HIST, EXC, ROWS), jnp.bfloat16),
            pltpu.VMEM((ROWS, NDEV * ROWS), jnp.bfloat16),
            pltpu.VMEM((EXC, ROWS), jnp.float32),
            pltpu.VMEM((ROWS, ROWS), jnp.float32),
            pltpu.VMEM((NDEV, EXC, ROWS), jnp.bfloat16),
            pltpu.VMEM((NDEV, EXC, ROWS), jnp.bfloat16),
            pltpu.SemaphoreType.DMA((6,)),
            pltpu.SemaphoreType.DMA,
            pltpu.SemaphoreType.DMA((len(GROUPS),)),
            pltpu.SemaphoreType.REGULAR((len(TELLERS),)),
        ],
        compiler_params=pltpu.CompilerParams(
            collective_id=0, has_side_effects=True, vmem_limit_bytes=40 << 20
        ),
    )(*args)


def solution(mesh):
    return jax.shard_map(
        per_device,
        mesh=mesh,
        in_specs=(
            P(None, None, ("blk", "grp")),
            P(("blk", "grp"), None),
            P(("blk", "grp"), None),
            P(("blk", "grp"), None),
            P(None, ("blk", "grp")),
            P(("blk", "grp"), None),
        ),
        out_specs=P(None, ("blk", "grp")),
        check_vma=False,
    )
```

```python
import jax
import jax.numpy as jnp
import numpy as np
from jax import lax
from jax.experimental import pallas as pl
from jax.experimental.pallas import tpu as pltpu
from jax.sharding import PartitionSpec as P

ORDER = 4
FRAC = 8
HIST = 96
EXC = 32
ROWS = 128
NDEV = 256
NX = 4
NY = 4
NZ = 8
MESH = pl.DeviceIdType.MESH


def hops(dx, dy, dz):
    return min(dx, NX - dx) + min(dy, NY - dy) + min(dz, NZ - dz)


PLANE = sorted(((dx, dy) for dx in range(NX) for dy in range(NY)), key=lambda d: hops(*d, 0))
CHIPS = [(dx, dy, dz) for dx, dy in PLANE for dz in range(NZ)]
FARTHEST = max(hops(*d) for d in CHIPS)
def make_plan():
    def long_way(d):
        return min(d[2], NZ - d[2])

    def ring(far, sign):
        return sorted((d for d in CHIPS if hops(*d) == far), key=lambda d: sign * long_way(d))

    return [ring(0, 1) + ring(1, -1), ring(2, -1), ring(3, 1) + ring(4, 1)[:14], ring(4, 1)[14:] + ring(5, 1) + ring(6, 1) + ring(7, 1) + ring(8, 1)]


LEAD = (2, 3, 4)
NEXT = ((1, 0, 0), (3, 0, 0), (0, 1, 0), (0, 3, 0), (0, 0, 1), (0, 0, 7))
TELLERS = (NEXT, NEXT, tuple(d for d in CHIPS if hops(*d) == 2), ((2, 2, 0), (0, 0, 4)))
PLAN = make_plan()
ORDERED = sum(PLAN, [])
assert sorted(ORDERED) == sorted(CHIPS)
SLOT = {d: 2 * n for n, d in enumerate(ORDERED)}
SIZES = (8, 20, 24, 24, 24, 16, 8, 4)
ENDS = [sum(SIZES[:n + 1]) for n in range(len(SIZES))]
GROUPS = [ORDERED[end - size:end] for size, end in zip(SIZES, ENDS)]
GROUP_OF = {d: n for n, group in enumerate(GROUPS) for d in group}
PARTS = ((0, 1), (2,), (3, 4))


def weight_table():
    fractions = np.arange(FRAC) / FRAC
    node_list = np.arange(ORDER) - (ORDER // 2 - 1)
    lagrange = np.ones((FRAC, ORDER))
    for column in range(ORDER):
        for partner in range(ORDER):
            if partner != column:
                lagrange[:, column] = (
                    lagrange[:, column]
                    * (fractions - node_list[partner])
                    / (node_list[column] - node_list[partner])
                )
    return lagrange.astype(np.float32)


def body(
    delays, offsets, history, kernel, incident, inverse, out,
    late, part_of, table, past, tiles, field, solve, send, recv,
    load_sem, send_sem, recv_sem, known_sem,
):
    blk = lax.axis_index("blk")
    grp = lax.axis_index("grp")
    z = blk % NZ
    x = grp // 4
    y = (blk // NZ) * 2 + (grp // 2) % 2
    c = grp % 2

    at_x = [((x + d) % NX) * 4 for d in range(NX)]
    ys = [(y + d) % NY for d in range(NY)]
    at_y = [((v // 2) * NZ, (v % 2) * 2) for v in ys]
    at_z = [(z + d) % NZ for d in range(NZ)]
    at_c = [c, 1 - c]

    def device(dx, dy, dz, dc):
        return at_y[dy][0] + at_z[dz], at_x[dx] + at_y[dy][1] + at_c[dc]

    def source_chip(dx, dy, dz):
        there = device(-dx % NX, -dy % NY, -dz % NZ, 0)
        return there[0] * 16 + there[1] - c

    def tell(sem, place):
        pl.semaphore_signal(sem, inc=1, device_id=device(*place), device_id_type=MESH)

    barrier = pltpu.get_barrier_semaphore()
    tell(barrier, (0, 0, 0, 1))
    for chip in NEXT:
        for dc in range(2):
            tell(barrier, (*chip, dc))

    loads = [
        pltpu.make_async_copy(source, target, load_sem.at[n])
        for n, (source, target) in enumerate(
            (
                (delays, late),
                (offsets, part_of),
                (history, past),
                (kernel, tiles),
                (incident, field),
                (inverse, solve),
            )
        )
    ]
    for load in loads:
        load.start()
    weights = weight_table()
    for s in range(FRAC):
        for p in range(ORDER):
            table[s, p] = jnp.float32(weights[s, p])
    for load in loads[:3]:
        load.wait()

    def interpolate(distances):
        plane = [d for d in PLANE if hops(*d, 0) in distances]

        def one_layer(dz, carry):
            for dx, dy in plane:
                for dc in range(2):
                    to = (at_y[dy][0] + (z + dz) % NZ) * 16 + at_x[dx] + at_y[dy][1] + at_c[dc]
                    first = late[0, to]
                    part = part_of[0, to]
                    total = table[part, 0] * past[first].astype(jnp.float32)
                    for p in range(1, ORDER):
                        total += table[part, p] * past[first + p].astype(jnp.float32)
                    send[((PLANE.index((dx, dy)) * NZ) + dz) * 2 + dc] = total.astype(jnp.bfloat16)
            return carry

        lax.fori_loop(0, NZ, one_layer, 0)

    lead_x = [jnp.minimum((x + d) % NX, 2) for d in range(NX)]
    lead_y = [jnp.minimum(v, 2) for v in ys]
    lead_z = [v + NZ * (v // 4) for v in at_z]

    def send_to(chip):
        for dc in range(2):
            if (*chip, dc) == (0, 0, 0, 0):
                continue
            start = (PLANE.index(chip[:2]) * NZ + chip[2]) * 2 + dc
            pltpu.make_async_remote_copy(
                src_ref=send.at[start],
                dst_ref=recv.at[SLOT[chip] + dc],
                send_sem=send_sem,
                recv_sem=recv_sem.at[GROUP_OF[chip]],
                device_id=device(*chip, dc),
                device_id_type=MESH,
            ).start()

    def ship(stage):
        if stage + 1 < len(PLAN):
            for chip in PLAN[stage]:
                send_to(chip)
            return
        for tier in range(len(LEAD) + 1):
            for chip in PLAN[stage]:
                dx, dy, dz = chip
                lead = lead_x[dx] + lead_y[dy] + lead_z[dz]
                if tier == 0:
                    ahead = lead <= LEAD[0]
                elif tier == len(LEAD):
                    ahead = lead > LEAD[-1]
                else:
                    ahead = jnp.logical_and(lead > LEAD[tier - 1], lead <= LEAD[tier])

                @pl.when(ahead)
                def _():
                    send_to(chip)

    for stage, tellers in enumerate(TELLERS):
        if stage < len(PARTS):
            interpolate(PARTS[stage])
        if stage == 0:
            recv[SLOT[0, 0, 0]] = send[0]
            pl.semaphore_wait(barrier, 2 * len(NEXT) + 1)
        else:
            pl.semaphore_wait(known_sem.at[stage], len(tellers))
        if stage + 1 < len(TELLERS):
            for chip in TELLERS[stage + 1]:
                tell(known_sem.at[stage + 1], (*chip, 0))
        ship(stage)

    for load in loads[3:]:
        load.wait()

    total = jnp.zeros((EXC, ROWS), jnp.float32)
    for n, chips in enumerate(GROUPS):
        own = 1 if (0, 0, 0) in chips else 0
        span = recv.at[pl.ds(SLOT[chips[0]] + own, 2 * len(chips) - own)]
        pltpu.make_async_copy(span, span, recv_sem.at[n]).wait()
        for chip in chips:
            low = recv[SLOT[chip] + c]
            high = recv[SLOT[chip] + 1 - c]
            column = pl.multiple_of(source_chip(*chip) * ROWS, 2 * ROWS)
            total += lax.dot_general(
                jnp.concatenate([low, high], axis=1),
                tiles[:, pl.ds(column, 2 * ROWS)],
                (((1,), (1,)), ((), ())),
                preferred_element_type=jnp.float32,
            )

    out[...] = lax.dot_general(
        field[...] - total,
        solve[...],
        (((1,), (1,)), ((), ())),
        precision=lax.Precision.HIGHEST,
        preferred_element_type=jnp.float32,
    )
    sent = send.at[pl.ds(1, NDEV - 1)]
    pltpu.make_async_copy(sent, sent, send_sem).wait()


def per_device(history, delays, offsets, kernel, incident, inverse):
    hbm = pl.BlockSpec(memory_space=pltpu.HBM)
    args = [
        pltpu.with_memory_space_constraint(a, pltpu.HBM)
        for a in (delays, offsets, history, kernel, incident, inverse)
    ]
    return pl.pallas_call(
        body,
        name="retarded_exchange",
        out_shape=jax.ShapeDtypeStruct((EXC, ROWS), jnp.float32),
        in_specs=[hbm] * 6,
        out_specs=pl.BlockSpec(memory_space=pltpu.VMEM),
        scratch_shapes=[
            pltpu.SMEM((1, NDEV), jnp.int32),
            pltpu.SMEM((1, NDEV), jnp.int32),
            pltpu.SMEM((FRAC, ORDER), jnp.float32),
            pltpu.VMEM((HIST, EXC, ROWS), jnp.bfloat16),
            pltpu.VMEM((ROWS, NDEV * ROWS), jnp.bfloat16),
            pltpu.VMEM((EXC, ROWS), jnp.float32),
            pltpu.VMEM((ROWS, ROWS), jnp.float32),
            pltpu.VMEM((NDEV, EXC, ROWS), jnp.bfloat16),
            pltpu.VMEM((NDEV, EXC, ROWS), jnp.bfloat16),
            pltpu.SemaphoreType.DMA((6,)),
            pltpu.SemaphoreType.DMA,
            pltpu.SemaphoreType.DMA((len(GROUPS),)),
            pltpu.SemaphoreType.REGULAR((len(TELLERS),)),
        ],
        compiler_params=pltpu.CompilerParams(
            collective_id=0, has_side_effects=True, vmem_limit_bytes=40 << 20
        ),
    )(*args)


def solution(mesh):
    return jax.shard_map(
        per_device,
        mesh=mesh,
        in_specs=(
            P(None, None, ("blk", "grp")),
            P(("blk", "grp"), None),
            P(("blk", "grp"), None),
            P(("blk", "grp"), None),
            P(None, ("blk", "grp")),
            P(("blk", "grp"), None),
        ),
        out_specs=P(None, ("blk", "grp")),
        check_vma=False,
    )
```
